512 devices in a mesh: row: 16 (over z_hi, y, core), col: 32 (over z_lo, x).
Axes of the slice: x: 4, y: 4, z: 16 (z_hi: 2, z_lo: 8; z = z_hi * 8 + z_lo), core: 2. Of those that a mesh axis runs over, the one named last changes fastest.
Arguments:
- tokens: bfloat16 [256, 8192], P('col', 'row'), may hold values from -6 to 6
- up_blocks: bfloat16 [16, 32, 7, 128, 128], P('row', 'col'), may hold values from -0.1875 to 0.1875
- up_index: int32 [16, 32, 7], P('row', 'col'), may hold values from 0 to 28, as said below
- down_blocks: bfloat16 [16, 32, 7, 128, 128], P('row', 'col'), may hold values from -0.09375 to 0.09375
- down_index: int32 [16, 32, 7], P('row', 'col'), may hold values from 0 to 28, as said below
- out_cot: bfloat16 [256, 8192], P('col', 'row'), may hold values from -1.5 to 1.5
Outputs:
- outputs: bfloat16 [256, 8192], P('col', 'row')
- input_grad: bfloat16 [256, 8192], P('col', 'row')
- up_grad: bfloat16 [16, 32, 7, 128, 128], P('row', 'col')
- down_grad: bfloat16 [16, 32, 7, 128, 128], P('row', 'col')
The draws below stay inside these ranges and needn't reach their ends.
Inputs may be any that keep to these rules, and one draw needn't show every extreme that they name: `up_index`: each entry names a block of its tile's 4 x 7 grid as row * 7 + column, or is 28 for an empty slot; the named blocks of a tile are distinct and come before its empty slots; every tile names at least one block; the tiles (r, c) with c * 16 // 32 == r name 7 blocks, every other tile fewer. `down_index`: each entry names a block of its tile's 7 x 4 grid (hidden-unit block, width block) as row * 4 + column, or is 28 for an empty slot; the named blocks of a tile are distinct and come before its empty slots; every tile names at least one block; the tiles (r, c) with c * 16 // 32 == r name 7 blocks, every other tile fewer.
All inputs are finite; a program needn't handle non-finite values.
Results may differ from the reference program's by a relative error of at most 0.023.
Values may be sent and summed in bfloat16 or wider, within the bound.
A program may use at most 64 MiB of HBM per device.

```python
import jax
import jax.numpy as jnp
from jax import lax

D = 8192
FF = 28672
BS = 128
GRID_R = 16
GRID_C = 32
TOKENS = 256
RB = 4
CB = 7
MOST = 7


def tile_pattern(key):
    count_all = RB * CB
    row_ids = jnp.arange(GRID_R, dtype=jnp.int32)[:, None]
    col_ids = jnp.arange(GRID_C, dtype=jnp.int32)[None, :]
    diagonal = col_ids * GRID_R // GRID_C == row_ids
    count_key, order_key = jax.random.split(key)
    counts = jax.random.randint(count_key, (GRID_R, GRID_C), 1, MOST, dtype=jnp.int32)
    counts = jnp.where(diagonal, MOST, counts)
    subkeys = jax.random.split(order_key, GRID_R * GRID_C)
    orders = jax.vmap(lambda subkey: jax.random.permutation(subkey, count_all))(subkeys)
    orders = orders.reshape(GRID_R, GRID_C, count_all)[:, :, :MOST].astype(jnp.int32)
    slots = jnp.arange(MOST, dtype=jnp.int32)
    return jnp.where(slots[None, None, :] < counts[:, :, None], orders, count_all).astype(jnp.int32)


def draw_up_index(key, part):
    return tile_pattern(jax.random.fold_in(key, 11))


def draw_down_index(key, part):
    return tile_pattern(jax.random.fold_in(key, 23))


def steps_of(rng, shape, cuts, low, top_value):
    def one(axis_at, blocks):
        draws = jax.random.uniform(jax.random.fold_in(jax.random.fold_in(rng, 6), axis_at), (blocks,), jnp.float32, low / len(cuts), top_value / len(cuts))
        return jnp.repeat(jnp.exp(draws), shape[axis_at] // blocks).reshape((-1,) + (1,) * (len(shape) - axis_at - 1))

    gain = one(*cuts[0])
    for cut in cuts[1:]:
        gain = gain * one(*cut)
    return gain


def normal_values(stream_key, extent, scale, most, cuts=(), kind=jnp.bfloat16):
    loudness = steps_of(stream_key, extent, cuts, -0.22, 0.18) if cuts else 1.0
    array = jax.random.normal(stream_key, extent, jnp.float32) * scale * loudness
    return jnp.minimum(jnp.maximum(array, -most), most).astype(kind)


def setup_inputs(seed: int = 0) -> dict:
    key_of = jax.random.split(jax.random.key(seed), 7)
    return {
        "tokens": normal_values(key_of[0], (TOKENS, D), 1.0, 6.0, ((0, 32), (1, 16))),
        "up_blocks": normal_values(key_of[1], (GRID_R, GRID_C, MOST, BS, BS), (D // 8) ** -0.5, 0.1875, ((0, 16), (1, 32))),
        "up_index": draw_up_index(jax.random.fold_in(key_of[6], 71), 0),
        "down_blocks": normal_values(key_of[3], (GRID_R, GRID_C, MOST, BS, BS), (FF // 8) ** -0.5, 0.09375, ((0, 16), (1, 32))),
        "down_index": draw_down_index(jax.random.fold_in(key_of[6], 71), 0),
        "out_cot": normal_values(key_of[5], (TOKENS, D), 0.25, 1.5, ((0, 32), (1, 16))),
    }


COEF = 0.7978845608
CUBIC = 0.044715


def gelu_value(values):
    inner = COEF * (values + CUBIC * values * values * values)
    return 0.5 * values * (1.0 + jnp.tanh(inner))


def gelu_slope(values):
    tangent = jnp.tanh(COEF * (values + CUBIC * values * values * values))
    return 0.5 * (1.0 + tangent) + 0.5 * values * (1.0 - tangent * tangent) * COEF * (1.0 + 3.0 * CUBIC * values * values)


def selectors(indices, leading, trailing):
    lead_pos = indices // trailing
    trail_pos = indices % trailing
    lead_sel = (lead_pos[:, None] == jnp.arange(leading, dtype=jnp.int32)[None, :]).astype(jnp.float32)
    trail_sel = (trail_pos[:, None] == jnp.arange(trailing, dtype=jnp.int32)[None, :]).astype(jnp.float32)
    return lead_sel, trail_sel


def forward_tile(operand, blocks, indices, leading, trailing):
    lead_sel, trail_sel = selectors(indices, leading, trailing)
    tok_count = operand.shape[0]
    pieces = operand.astype(jnp.float32).reshape(tok_count, leading, BS)
    picked = jnp.einsum('tab,ka->ktb', pieces, lead_sel, precision=lax.Precision.HIGHEST)
    products = jnp.einsum('ktb,kbd->ktd', picked, blocks.astype(jnp.float32), precision=lax.Precision.HIGHEST)
    result = jnp.einsum('ktd,kc->tcd', products, trail_sel, precision=lax.Precision.HIGHEST)
    return result.reshape(tok_count, trailing * BS)


def backward_tile(other, blocks, indices, leading, trailing):
    lead_sel, trail_sel = selectors(indices, leading, trailing)
    tok_count = other.shape[0]
    pieces = other.astype(jnp.float32).reshape(tok_count, trailing, BS)
    picked = jnp.einsum('tcd,kc->ktd', pieces, trail_sel, precision=lax.Precision.HIGHEST)
    products = jnp.einsum('ktd,kbd->ktb', picked, blocks.astype(jnp.float32), precision=lax.Precision.HIGHEST)
    result = jnp.einsum('ktb,ka->tab', products, lead_sel, precision=lax.Precision.HIGHEST)
    return result.reshape(tok_count, leading * BS)


def grad_tile(operand, other, indices, leading, trailing):
    lead_sel, trail_sel = selectors(indices, leading, trailing)
    tok_count = operand.shape[0]
    left_pick = jnp.einsum('tab,ka->ktb', operand.astype(jnp.float32).reshape(tok_count, leading, BS), lead_sel, precision=lax.Precision.HIGHEST)
    right_pick = jnp.einsum('tcd,kc->ktd', other.astype(jnp.float32).reshape(tok_count, trailing, BS), trail_sel, precision=lax.Precision.HIGHEST)
    return jnp.einsum('ktb,ktd->kbd', left_pick, right_pick, precision=lax.Precision.HIGHEST)


def rounded(values):
    return lax.optimization_barrier(values.astype(jnp.bfloat16)).astype(jnp.float32)


def reference(tokens, up_blocks, up_index, down_blocks, down_index, out_cot):
    tok_count = tokens.shape[0]
    by_row = tokens.reshape(tok_count, GRID_R, RB * BS).transpose(1, 0, 2)
    cot_by_row = out_cot.reshape(tok_count, GRID_R, RB * BS).transpose(1, 0, 2)
    up_by_col = jnp.swapaxes(up_blocks, 0, 1)
    up_index_col = jnp.swapaxes(up_index, 0, 1)
    down_by_col = jnp.swapaxes(down_blocks, 0, 1)
    down_index_col = jnp.swapaxes(down_index, 0, 1)

    def up_step(running, inputs):
        feats, blocks_row, index_row = inputs
        terms = jax.vmap(lambda blk, ind: forward_tile(feats, blk, ind, RB, CB))(blocks_row, index_row)
        return running + rounded(terms), None

    preact, _ = lax.scan(up_step, jnp.zeros((GRID_C, tok_count, CB * BS), jnp.float32), (by_row, up_blocks, up_index))
    hidden = gelu_value(preact).astype(jnp.bfloat16)

    def down_step(running, inputs):
        hidden_col, blocks_col, index_col = inputs
        terms = jax.vmap(lambda blk, ind: forward_tile(hidden_col, blk, ind, CB, RB))(blocks_col, index_col)
        return running + rounded(terms), None

    out_sum, _ = lax.scan(down_step, jnp.zeros((GRID_R, tok_count, RB * BS), jnp.float32), (hidden, down_by_col, down_index_col))
    outputs = out_sum.transpose(1, 0, 2).reshape(tok_count, D).astype(jnp.bfloat16)

    def act_step(running, inputs):
        cot_row, blocks_row, index_row = inputs
        terms = jax.vmap(lambda blk, ind: backward_tile(cot_row, blk, ind, CB, RB))(blocks_row, index_row)
        return running + rounded(terms), None

    act_grad, _ = lax.scan(act_step, jnp.zeros((GRID_C, tok_count, CB * BS), jnp.float32), (cot_by_row, down_blocks, down_index))
    pre_grad = (act_grad * gelu_slope(preact)).astype(jnp.bfloat16)

    def input_step(running, inputs):
        grad_col, blocks_col, index_col = inputs
        terms = jax.vmap(lambda blk, ind: backward_tile(grad_col, blk, ind, RB, CB))(blocks_col, index_col)
        return running + rounded(terms), None

    in_sum, _ = lax.scan(input_step, jnp.zeros((GRID_R, tok_count, RB * BS), jnp.float32), (pre_grad, up_by_col, up_index_col))
    input_grad = in_sum.transpose(1, 0, 2).reshape(tok_count, D).astype(jnp.bfloat16)

    def up_grad_row(inputs):
        feats, index_row = inputs
        return jax.vmap(lambda grad_col, ind: grad_tile(feats, grad_col, ind, RB, CB))(pre_grad, index_row)

    up_grad = lax.map(up_grad_row, (by_row, up_index)).astype(jnp.bfloat16)

    def down_grad_row(inputs):
        cot_row, index_row = inputs
        return jax.vmap(lambda hidden_col, ind: grad_tile(hidden_col, cot_row, ind, CB, RB))(hidden, index_row)

    down_grad = lax.map(down_grad_row, (cot_by_row, down_index)).astype(jnp.bfloat16)
    return (outputs, input_grad, up_grad, down_grad)
```

```python
import functools

import jax
import jax.numpy as jnp
from jax import lax
from jax.experimental import pallas as pl
from jax.experimental.pallas import tpu as pltpu
from jax.sharding import PartitionSpec as P

MESH = pl.DeviceIdType.MESH
BF16 = jnp.bfloat16
F32 = jnp.float32

BS = 128
NX = 4
NY = 4
NC = 2

COEF = 0.7978845608
CUBIC = 0.044715


def body(
    dims,
    tok_ref,
    cot_ref,
    up_idx,
    down_idx,
    up_hbm,
    down_hbm,
    out_ref,
    ing_ref,
    upg_hbm,
    downg_hbm,
    up_blk,
    down_blk,
    w1,
    w2,
    tok_all,
    cot_all,
    feats,
    cots,
    term,
    r1,
    half,
    r2,
    share,
    r3,
    hid,
    xterm,
    e1,
    zsum,
    e2,
    gdense,
    gout,
    local_sem,
    send_sem,
    recv_sem,
):
    nz, nx, nzh, ny, nc, rb, cb, slots = dims
    row = lax.axis_index("row")
    col = lax.axis_index("col")
    core = row % nc
    y = (row // nc) % ny
    zh = row // (nc * ny)
    x = col % nx
    z = col // nx
    tok_count = nz * nx * tok_ref.shape[0]
    wide = rb * BS
    tall = cb * BS

    def row_of(zh_, y_, core_):
        return (zh_ * ny + y_) * nc + core_

    def z_dev(k):
        return (row, ((z + k) % nz) * nx + x)

    def x_dev(k):
        return (row, z * nx + (x + k) % nx)

    def y_dev(k):
        return (row_of(zh, (y + k) % ny, core), col)

    core_dev = (row_of(zh, y, 1 - core), col)
    zh_dev = (row_of(1 - zh, y, core), col)

    partners = [z_dev(k) for k in range(1, nz)] + [x_dev(k) for k in range(1, nx)]
    partners += [y_dev(k) for k in range(1, ny)] + [core_dev, zh_dev]

    count = [0]
    started = []

    def send(src, dst, device):
        at = count[0]
        count[0] += 1
        copy = pltpu.make_async_remote_copy(
            src_ref=src,
            dst_ref=dst,
            send_sem=send_sem.at[at],
            recv_sem=recv_sem.at[at],
            device_id=device,
            device_id_type=MESH,
        )
        copy.start()
        started.append(copy)
        return copy

    up_load = pltpu.make_async_copy(up_hbm.at[0, 0], up_blk.at[pl.ds(0, slots)], local_sem.at[0])
    down_load = pltpu.make_async_copy(
        down_hbm.at[0, 0], down_blk.at[pl.ds(0, slots)], local_sem.at[1]
    )
    up_load.start()
    down_load.start()

    barrier = pltpu.get_barrier_semaphore()
    for device in partners:
        pl.semaphore_signal(barrier, inc=1, device_id=device, device_id_type=MESH)
    pl.semaphore_wait(barrier, len(partners))

    gather_z = []
    for own, full in ((tok_ref, tok_all), (cot_ref, cot_all)):
        gather_z.append([send(own, full.at[0, k], z_dev(k)) for k in range(1, nz)])
        full[0, 0] = own[...]

    for load, blk, index, dense, leading, trailing in (
        (up_load, up_blk, up_idx, w1, rb, cb),
        (down_load, down_blk, down_idx, w2, cb, rb),
    ):
        blk[slots] = jnp.zeros((BS, BS), BF16)
        load.wait()
        entries = [index[0, 0, k] for k in range(slots)]
        for place in range(leading * trailing):
            slot = jnp.int32(slots)
            for k in range(slots):
                slot = jnp.where(entries[k] == place, jnp.int32(k), slot)
            a, b = place // trailing, place % trailing
            dense[a * BS : (a + 1) * BS, b * BS : (b + 1) * BS] = blk[slot]

    gather_x = []
    for copies, full in zip(gather_z, (tok_all, cot_all)):
        for copy in copies:
            copy.wait_recv()
        gather_x.append([send(full.at[0], full.at[k], x_dev(k)) for k in range(1, nx)])

    per_x = tok_count // nx
    parts = nc * ny
    rows = tok_count // parts
    to_core = []
    for s, (copies, full, flat) in enumerate(
        zip(gather_x, (tok_all, cot_all), (feats, cots))
    ):
        for copy in copies:
            copy.wait_recv()
        for k in range(nx):
            flat[k * per_x : (k + 1) * per_x, :] = (
                full[k].astype(F32).reshape(per_x, wide).astype(BF16)
            )
        if s == 0:
            value = jnp.dot(flat[...], w1[...], preferred_element_type=F32)
        else:
            value = lax.dot_general(
                flat[...], w2[...], (((1,), (1,)), ((), ())), preferred_element_type=F32
            )
        term[s] = value.astype(BF16).reshape(parts, rows, tall)
        to_core.append(
            send(term.at[s, pl.ds((1 - core) * ny, ny)], r1.at[s], core_dev)
        )

    to_y = []
    for s in range(2):
        to_core[s].wait_recv()
        half[s] = (
            term[s, pl.ds(core * ny, ny)].astype(F32) + r1[s].astype(F32)
        ).astype(BF16)
        to_y.append(
            [send(half.at[s, (y + k) % ny], r2.at[s, k - 1], y_dev(k)) for k in range(1, ny)]
        )
    to_zh = []
    for s in range(2):
        for copy in to_y[s]:
            copy.wait_recv()
        total = half[s, y].astype(F32)
        for k in range(1, ny):
            total = total + r2[s, k - 1].astype(F32)
        share[s] = total.astype(BF16)
        to_zh.append(send(share.at[s], r3.at[s], zh_dev))

    mine = core * ny + y
    to_zh[0].wait_recv()
    v = share[0].astype(F32) + r3[0].astype(F32)
    t = jnp.tanh(COEF * (v + CUBIC * v * v * v))
    hid[0, mine] = (0.5 * v * (1.0 + t)).astype(BF16)
    spread_y = [[send(hid.at[0, mine], hid.at[0, mine], y_dev(k)) for k in range(1, ny)]]
    slope = 0.5 * (1.0 + t) + 0.5 * v * (1.0 - t * t) * COEF * (1.0 + 3.0 * CUBIC * v * v)
    to_zh[1].wait_recv()
    act = share[1].astype(F32) + r3[1].astype(F32)
    hid[1, mine] = (act * slope).astype(BF16)
    spread_y.append([send(hid.at[1, mine], hid.at[1, mine], y_dev(k)) for k in range(1, ny)])
    spread_core = []
    for s in range(2):
        for copy in spread_y[s]:
            copy.wait_recv()
        mine_half = pl.ds(core * ny, ny)
        spread_core.append(send(hid.at[s, mine_half], hid.at[s, mine_half], core_dev))

    to_x = []
    for s in range(2):
        spread_core[s].wait_recv()
        value = hid[s].reshape(tok_count, tall)
        if s == 0:
            part = jnp.dot(value, w2[...], preferred_element_type=F32)
        else:
            part = lax.dot_general(
                value, w1[...], (((1,), (1,)), ((), ())), preferred_element_type=F32
            )
        xterm[s] = part.reshape(nx, nz, per_x // nz, wide).astype(BF16)
        to_x.append([send(xterm.at[s, k], e1.at[s, k - 1], x_dev(nx - k)) for k in range(1, nx)])

    def grads(s):
        if s == 0:
            left, right = feats[...], hid[1].reshape(tok_count, tall)
        else:
            left, right = hid[0].reshape(tok_count, tall), cots[...]
        full = lax.dot_general(left, right, (((0,), (0,)), ((), ())), preferred_element_type=F32)
        trailing = (cb, rb)[s]
        for place in range(rb * cb):
            a, b = place // trailing, place % trailing
            gdense[s, place] = full[a * BS : (a + 1) * BS, b * BS : (b + 1) * BS].astype(BF16)
        gdense[s, rb * cb] = jnp.zeros((BS, BS), BF16)
        index = (up_idx, down_idx)[s]
        for k in range(slots):
            gout[s, k] = gdense[s, index[0, 0, k]]
        copy = pltpu.make_async_copy(
            gout.at[s], (upg_hbm, downg_hbm)[s].at[0, 0], local_sem.at[2 + s]
        )
        copy.start()
        return copy

    writes = [grads(0)]
    to_z = []
    for s in range(2):
        for copy in to_x[s]:
            copy.wait_recv()
        total = xterm[s, 0].astype(F32)
        for k in range(1, nx):
            total = total + e1[s, k - 1].astype(F32)
        zsum[s] = total.astype(BF16)
        to_z.append([send(zsum.at[s, k], e2.at[s, k - 1], z_dev(nz - k)) for k in range(1, nz)])
    writes.append(grads(1))
    for s, ref in enumerate((out_ref, ing_ref)):
        for copy in to_z[s]:
            copy.wait_recv()
        total = zsum[s, 0].astype(F32)
        for k in range(1, nz):
            total = total + e2[s, k - 1].astype(F32)
        ref[...] = total.astype(BF16)
    for copy in writes:
        copy.wait()
    for copy in started:
        copy.wait_send()


def shards(tokens, up_blocks, up_index, down_blocks, down_index, out_cot):
    own, wide = tokens.shape
    slots = up_blocks.shape[2]
    rb = wide // BS
    nx, ny, nc = NX, NY, NC
    nz = lax.axis_size("col") // nx
    nzh = lax.axis_size("row") // (ny * nc)
    cb = 7
    tall = cb * BS
    tok_count = own * nz * nx
    parts = ny * nc
    rows = tok_count // parts
    n_copies = 2 * (nz - 1 + nx - 1 + 1 + ny - 1 + 1 + ny - 1 + 1 + nx - 1 + nz - 1)
    vmem = pl.BlockSpec(memory_space=pltpu.VMEM)
    smem = pl.BlockSpec(memory_space=pltpu.SMEM)
    hbm = pl.BlockSpec(memory_space=pl.ANY)
    blocks_shape = jax.ShapeDtypeStruct(up_blocks.shape, BF16)
    small = jax.ShapeDtypeStruct((own, wide), BF16)
    return pl.pallas_call(
        functools.partial(body, (nz, nx, nzh, ny, nc, rb, cb, slots)),
        out_shape=(small, small, blocks_shape, blocks_shape),
        in_specs=[vmem, vmem, smem, smem, hbm, hbm],
        out_specs=(vmem, vmem, hbm, hbm),
        scratch_shapes=[
            pltpu.VMEM((slots + 1, BS, BS), BF16),
            pltpu.VMEM((slots + 1, BS, BS), BF16),
            pltpu.VMEM((wide, tall), BF16),
            pltpu.VMEM((tall, wide), BF16),
            pltpu.VMEM((nx, nz, own, wide), BF16),
            pltpu.VMEM((nx, nz, own, wide), BF16),
            pltpu.VMEM((tok_count, wide), BF16),
            pltpu.VMEM((tok_count, wide), BF16),
            pltpu.VMEM((2, parts, rows, tall), BF16),
            pltpu.VMEM((2, ny, rows, tall), BF16),
            pltpu.VMEM((2, ny, rows, tall), BF16),
            pltpu.VMEM((2, ny - 1, rows, tall), BF16),
            pltpu.VMEM((2, rows, tall), BF16),
            pltpu.VMEM((2, rows, tall), BF16),
            pltpu.VMEM((2, parts, rows, tall), BF16),
            pltpu.VMEM((2, nx, nz, own, wide), BF16),
            pltpu.VMEM((2, nx - 1, nz, own, wide), BF16),
            pltpu.VMEM((2, nz, own, wide), BF16),
            pltpu.VMEM((2, nz - 1, own, wide), BF16),
            pltpu.VMEM((2, rb * cb + 1, BS, BS), BF16),
            pltpu.VMEM((2, slots, BS, BS), BF16),
            pltpu.SemaphoreType.DMA((4,)),
            pltpu.SemaphoreType.DMA((n_copies,)),
            pltpu.SemaphoreType.DMA((n_copies,)),
        ],
        compiler_params=pltpu.CompilerParams(
            collective_id=0, has_side_effects=True, vmem_limit_bytes=48 << 20
        ),
    )(tokens, out_cot, up_index, down_index, up_blocks, down_blocks)


def solution(mesh):
    placed = (
        P("col", "row"),
        P("row", "col", None, None, None),
        P("row", "col", None),
        P("row", "col", None, None, None),
        P("row", "col", None),
        P("col", "row"),
    )
    return jax.shard_map(
        shards,
        mesh=mesh,
        in_specs=placed,
        out_specs=(
            P("col", "row"),
            P("col", "row"),
            P("row", "col", None, None, None),
            P("row", "col", None, None, None),
        ),
        check_vma=False,
    )
```

```python
import functools

import jax
import jax.numpy as jnp
from jax import lax
from jax.experimental import pallas as pl
from jax.experimental.pallas import tpu as pltpu
from jax.sharding import PartitionSpec as P

MESH = pl.DeviceIdType.MESH
BF16 = jnp.bfloat16
F32 = jnp.float32

BS = 128
CB = 7
NX = 4
NZ = 8
NY = 4
NC = 2
HZ = NZ // 2
NEAR, FAR = 0, 1

COEF = 0.7978845608
CUBIC = 0.044715


def body(
    tok_hbm,
    cot_hbm,
    up_idx_hbm,
    down_idx_hbm,
    up_hbm,
    down_hbm,
    out_hbm,
    ing_hbm,
    upg_hbm,
    downg_hbm,
    up_blk,
    down_blk,
    w1,
    w2,
    gathered,
    flat,
    term,
    r1,
    half,
    r2,
    share,
    r3,
    hid,
    xterm,
    e1,
    zsum,
    e2,
    gdense,
    gout,
    final,
    up_idx,
    down_idx,
    local_sem,
    send_sem,
    gz_sem,
    gx_sem,
    c1_sem,
    c2_sem,
    c3_sem,
    c4_sem,
    c5_sem,
    e1_sem,
    e2_sem,
):
    own, wide = tok_hbm.shape
    slots = up_hbm.shape[2]
    rb = wide // BS
    cb = CB
    tall = cb * BS
    per_half = HZ * NX * own
    row = lax.axis_index("row")
    col = lax.axis_index("col")
    core = row % NC
    y = (row // NC) % NY
    zh = row // (NC * NY)
    x = col % NX
    z = col // NX
    side = z // HZ
    q = z % HZ
    base = (side * HZ, (1 - side) * HZ)
    near = (side * HZ + q + 1 - 2 * (q % 2), side * HZ + q + 2 - 4 * (q // 2), side * HZ + 3 - q)
    far = tuple(HZ + j - side * (1 + 2 * j) for j in range(HZ))

    def row_of(zh_, y_, core_):
        return (zh_ * NY + y_) * NC + core_

    def z_dev(z_):
        return (row, z_ * NX + x)

    def x_dev(k):
        return (row, z * NX + (x + k) % NX)

    def y_dev(k):
        return (row_of(zh, (y + k) % NY, core), col)

    core_dev = (row_of(zh, y, 1 - core), col)
    zh_dev = (row_of(1 - zh, y, core), col)

    partners = [z_dev(p) for p in far + near] + [x_dev(k) for k in range(1, NX)]
    partners += [y_dev(k) for k in range(1, NY)] + [core_dev, zh_dev]

    barrier = pltpu.get_barrier_semaphore()
    for device in [zh_dev] + partners[:-1]:
        pl.semaphore_signal(barrier, inc=1, device_id=device, device_id_type=MESH)

    started = []

    def send(src, dst, sem, device):
        copy = pltpu.make_async_remote_copy(
            src_ref=src,
            dst_ref=dst,
            send_sem=send_sem.at[len(started)],
            recv_sem=sem,
            device_id=device,
            device_id_type=MESH,
        )
        copy.start()
        started.append(copy)

    def arrived(dst, sem):
        pltpu.make_async_remote_copy(
            src_ref=dst,
            dst_ref=dst,
            send_sem=send_sem.at[0],
            recv_sem=sem,
            device_id=core_dev,
            device_id_type=MESH,
        ).wait_recv()

    def load(at, src, dst):
        copy = pltpu.make_async_copy(src, dst, local_sem.at[at])
        copy.start()
        return copy

    tok_load = load(0, tok_hbm, gathered.at[0, z, 0])
    cot_load = load(1, cot_hbm, gathered.at[0, z, 1])
    up_idx_load = load(2, up_idx_hbm, up_idx)
    down_idx_load = load(3, down_idx_hbm, down_idx)
    up_load = load(4, up_hbm.at[0, 0], up_blk.at[pl.ds(0, slots)])
    down_load = load(5, down_hbm.at[0, 0], down_blk.at[pl.ds(0, slots)])

    for idx_load, blk_load, blk, index, dense, leading, trailing in (
        (up_idx_load, up_load, up_blk, up_idx, w1, rb, cb),
        (down_idx_load, down_load, down_blk, down_idx, w2, cb, rb),
    ):
        blk[slots] = jnp.zeros((BS, BS), BF16)
        idx_load.wait()
        blk_load.wait()
        entries = [index[0, 0, k] for k in range(slots)]
        for place in range(leading * trailing):
            slot = jnp.int32(slots)
            for k in range(slots):
                slot = jnp.where(entries[k] == place, jnp.int32(k), slot)
            a, b = place // trailing, place % trailing
            dense[a * BS : (a + 1) * BS, b * BS : (b + 1) * BS] = blk[slot]

    tok_load.wait()
    cot_load.wait()
    with jax.named_scope("w_barrier"):
        pl.semaphore_wait(barrier, len(partners))

    for p in far[::-1] + near[::-1]:
        send(gathered.at[0, z], gathered.at[0, z], gz_sem.at[z], z_dev(p))

    def forward(p):
        for k in range(1, NX):
            send(gathered.at[0, p], gathered.at[k, p], gx_sem.at[k - 1, p], x_dev(k))

    forward(z)
    for j, places in ((NEAR, near), (FAR, far)):
        for p in places:
            with jax.named_scope(f"w_gz{j}"):
                arrived(gathered.at[0, p], gz_sem.at[p])
            forward(p)

    def terms(j):
        with jax.named_scope(f"w_gx{j}"):
            for k in range(1, NX):
                for i in range(HZ):
                    p = base[j] + i
                    arrived(gathered.at[k, p], gx_sem.at[k - 1, p])
        for s in range(2):
            for k in range(NX):
                flat[s, j, k * HZ * own : (k + 1) * HZ * own, :] = (
                    gathered[k, pl.ds(base[j], HZ), s]
                    .astype(F32)
                    .reshape(HZ * own, wide)
                    .astype(BF16)
                )
            if s == 0:
                value = jnp.dot(flat[s, j], w1[...], preferred_element_type=F32)
            else:
                value = lax.dot_general(
                    flat[s, j], w2[...], (((1,), (1,)), ((), ())), preferred_element_type=F32
                )
            term[j, s] = value.astype(BF16).reshape(term.shape[2:])
            send(term.at[j, s, pl.ds((1 - core) * NY, NY)], r1.at[j, s], c1_sem.at[j, s], core_dev)

    def to_y(j, s):
        with jax.named_scope(f"w_c1_{j}{s}"):
            arrived(r1.at[j, s], c1_sem.at[j, s])
        half[j, s] = (
            term[j, s, pl.ds(core * NY, NY)].astype(F32) + r1[j, s].astype(F32)
        ).astype(BF16)
        for k in range(1, NY):
            send(half.at[j, s, (y + k) % NY], r2.at[j, s, k - 1], c2_sem.at[j, s, k - 1], y_dev(k))

    def to_zh(j, s):
        with jax.named_scope(f"w_c2_{j}{s}"):
            for k in range(1, NY):
                arrived(r2.at[j, s, k - 1], c2_sem.at[j, s, k - 1])
        total = half[j, s, y].astype(F32)
        for k in range(1, NY):
            total = total + r2[j, s, k - 1].astype(F32)
        share[j, s] = total.astype(BF16)
        send(share.at[j, s], r3.at[j, s], c3_sem.at[j, s], zh_dev)

    mine = core * NY + y

    def shared(j, s):
        with jax.named_scope(f"w_c3_{j}{s}"):
            arrived(r3.at[j, s], c3_sem.at[j, s])
        return share[j, s].astype(F32) + r3[j, s].astype(F32)

    def spread(j, s):
        if s == 0:
            v = shared(j, 0)
            t = jnp.tanh(COEF * (v + CUBIC * v * v * v))
            hid[j, s, mine] = (0.5 * v * (1.0 + t)).astype(BF16)
        else:
            act = shared(j, 1)
            v = share[j, 0].astype(F32) + r3[j, 0].astype(F32)
            t = jnp.tanh(COEF * (v + CUBIC * v * v * v))
            slope = 0.5 * (1.0 + t) + 0.5 * v * (1.0 - t * t) * COEF * (1.0 + 3.0 * CUBIC * v * v)
            hid[j, s, mine] = (act * slope).astype(BF16)
        for k in range(1, NY):
            send(hid.at[j, s, mine], hid.at[j, s, mine], c4_sem.at[j, s, k - 1], y_dev(k))

    def to_core(j, s):
        with jax.named_scope(f"w_c4_{j}{s}"):
            for k in range(1, NY):
                place = core * NY + (y - k) % NY
                arrived(hid.at[j, s, place], c4_sem.at[j, s, k - 1])
        places = pl.ds(core * NY, NY)
        send(hid.at[j, s, places], hid.at[j, s, places], c5_sem.at[j, s], core_dev)

    def to_x(j, s):
        with jax.named_scope(f"w_c5_{j}{s}"):
            arrived(hid.at[j, s, pl.ds((1 - core) * NY, NY)], c5_sem.at[j, s])
        value = hid[j, s].reshape(per_half, tall)
        if s == 0:
            part = jnp.dot(value, w2[...], preferred_element_type=F32)
        else:
            part = lax.dot_general(
                value, w1[...], (((1,), (1,)), ((), ())), preferred_element_type=F32
            )
        xterm[j, s] = part.reshape(NX, HZ, own, wide).astype(BF16)
        for k in range(1, NX):
            send(xterm.at[j, s, k], e1.at[j, s, k - 1], e1_sem.at[j, s, k - 1], x_dev(NX - k))

    def to_z(j, s):
        with jax.named_scope(f"w_e1_{j}{s}"):
            for k in range(1, NX):
                arrived(e1.at[j, s, k - 1], e1_sem.at[j, s, k - 1])
        total = xterm[j, s, 0].astype(F32)
        for k in range(1, NX):
            total = total + e1[j, s, k - 1].astype(F32)
        zsum[j, s] = total.astype(BF16)
        for p in (near, far)[j][::-1]:
            send(zsum.at[j, s, p % HZ], e2.at[s, z], e2_sem.at[s, z], z_dev(p))
        if j == NEAR:
            e2[s, z] = zsum[j, s, q]

    def grads(s):
        if s == 0:
            left = flat[0].reshape(2 * per_half, wide)
            right = hid[:, 1].reshape(2 * per_half, tall)
        else:
            left = hid[:, 0].reshape(2 * per_half, tall)
            right = flat[1].reshape(2 * per_half, wide)
        full = lax.dot_general(left, right, (((0,), (0,)), ((), ())), preferred_element_type=F32)
        trailing = (cb, rb)[s]
        for place in range(rb * cb):
            a, b = place // trailing, place % trailing
            gdense[s, place] = full[a * BS : (a + 1) * BS, b * BS : (b + 1) * BS].astype(BF16)
        gdense[s, rb * cb] = jnp.zeros((BS, BS), BF16)
        index = (up_idx, down_idx)[s]
        for k in range(slots):
            gout[s, k] = gdense[s, index[0, 0, k]]
        return load(6 + s, gout.at[s], (upg_hbm, downg_hbm)[s].at[0, 0])

    terms(NEAR)
    to_y(NEAR, 0)
    to_y(NEAR, 1)
    terms(FAR)
    to_y(FAR, 0)
    to_y(FAR, 1)
    to_zh(NEAR, 0)
    to_zh(NEAR, 1)
    to_zh(FAR, 0)
    to_zh(FAR, 1)
    spread(NEAR, 0)
    spread(NEAR, 1)
    to_core(NEAR, 0)
    spread(FAR, 0)
    to_core(NEAR, 1)
    to_x(NEAR, 0)
    spread(FAR, 1)
    to_x(NEAR, 1)
    to_core(FAR, 0)
    to_x(FAR, 0)
    to_core(FAR, 1)
    to_x(FAR, 1)
    to_z(FAR, 0)
    with jax.named_scope("grads1"):
        writes = [grads(1)]
    to_z(FAR, 1)
    to_z(NEAR, 0)
    to_z(NEAR, 1)
    with jax.named_scope("grads0"):
        writes.append(grads(0))
    for s, ref in enumerate((out_hbm, ing_hbm)):
        with jax.named_scope(f"w_e2_{s}"):
            for p in near + far:
                arrived(e2.at[s, p], e2_sem.at[s, p])
        total = e2[s, 0].astype(F32)
        for p in range(1, NZ):
            total = total + e2[s, p].astype(F32)
        final[s] = total.astype(BF16)
        writes.append(load(8 + s, final.at[s], ref))
    for copy in writes:
        copy.wait()
    for copy in started:
        copy.wait_send()


def hand_over(*refs):
    sources, targets, bounce, sem = refs[:4], refs[4:8], refs[8:12], refs[12]
    order = (2, 3, 0, 1)
    loads = {i: pltpu.make_async_copy(sources[i], bounce[i], sem.at[0, i]) for i in order}
    stores = {i: pltpu.make_async_copy(bounce[i], targets[i], sem.at[1, i]) for i in order}
    for i in order:
        loads[i].start()
    for i in order:
        loads[i].wait()
        stores[i].start()
    for i in order:
        stores[i].wait()


def shards(tokens, up_blocks, up_index, down_blocks, down_index, out_cot):
    own, wide = tokens.shape
    slots = up_blocks.shape[2]
    rb = wide // BS
    tall = CB * BS
    parts = NC * NY
    rows = HZ * NX * own // parts
    n_copies = NZ - 1 + NZ * (NX - 1) + 4 * (1 + NY - 1 + 1 + NY - 1 + 1 + NX - 1) + 2 * (NZ - 1)
    hbm = pl.BlockSpec(memory_space=pltpu.HBM)
    blocks_shape = jax.ShapeDtypeStruct(up_blocks.shape, BF16)
    small = jax.ShapeDtypeStruct((own, wide), BF16)
    dma = pltpu.SemaphoreType.DMA
    results = pl.pallas_call(
        body,
        out_shape=(small, small, blocks_shape, blocks_shape),
        in_specs=[hbm] * 6,
        out_specs=(hbm,) * 4,
        scratch_shapes=[
            pltpu.VMEM((slots + 1, BS, BS), BF16),
            pltpu.VMEM((slots + 1, BS, BS), BF16),
            pltpu.VMEM((wide, tall), BF16),
            pltpu.VMEM((tall, wide), BF16),
            pltpu.VMEM((NX, NZ, 2, own, wide), BF16),
            pltpu.VMEM((2, 2, HZ * NX * own, wide), BF16),
            pltpu.VMEM((2, 2, parts, rows, tall), BF16),
            pltpu.VMEM((2, 2, NY, rows, tall), BF16),
            pltpu.VMEM((2, 2, NY, rows, tall), BF16),
            pltpu.VMEM((2, 2, NY - 1, rows, tall), BF16),
            pltpu.VMEM((2, 2, rows, tall), BF16),
            pltpu.VMEM((2, 2, rows, tall), BF16),
            pltpu.VMEM((2, 2, parts, rows, tall), BF16),
            pltpu.VMEM((2, 2, NX, HZ, own, wide), BF16),
            pltpu.VMEM((2, 2, NX - 1, HZ, own, wide), BF16),
            pltpu.VMEM((2, 2, HZ, own, wide), BF16),
            pltpu.VMEM((2, NZ, own, wide), BF16),
            pltpu.VMEM((2, rb * CB + 1, BS, BS), BF16),
            pltpu.VMEM((2, slots, BS, BS), BF16),
            pltpu.VMEM((2, own, wide), BF16),
            pltpu.SMEM(up_index.shape, jnp.int32),
            pltpu.SMEM(down_index.shape, jnp.int32),
            dma((10,)),
            dma((n_copies,)),
            dma((NZ,)),
            dma((NX - 1, NZ)),
            dma((2, 2)),
            dma((2, 2, NY - 1)),
            dma((2, 2)),
            dma((2, 2, NY - 1)),
            dma((2, 2)),
            dma((2, 2, NX - 1)),
            dma((2, NZ)),
        ],
        compiler_params=pltpu.CompilerParams(collective_id=0, has_side_effects=True),
    )(tokens, out_cot, up_index, down_index, up_blocks, down_blocks)
    return pl.pallas_call(
        hand_over,
        out_shape=(small, small, blocks_shape, blocks_shape),
        in_specs=[hbm] * 4,
        out_specs=(hbm,) * 4,
        scratch_shapes=[
            pltpu.VMEM(small.shape, BF16),
            pltpu.VMEM(small.shape, BF16),
            pltpu.VMEM(blocks_shape.shape, BF16),
            pltpu.VMEM(blocks_shape.shape, BF16),
            dma((2, 4)),
        ],
    )(*results)


def solution(mesh):
    placed = (
        P("col", "row"),
        P("row", "col", None, None, None),
        P("row", "col", None),
        P("row", "col", None, None, None),
        P("row", "col", None),
        P("col", "row"),
    )
    return jax.shard_map(
        shards,
        mesh=mesh,
        in_specs=placed,
        out_specs=(
            P("col", "row"),
            P("col", "row"),
            P("row", "col", None, None, None),
            P("row", "col", None, None, None),
        ),
        check_vma=False,
    )
```
